32 devices in a mesh: groups: 2 (over x), cent: 16 (over z, y, core).
Axes of the slice: x: 2, y: 2, z: 4, core: 2. Of those that a mesh axis runs over, the one named last changes fastest.
Arguments:
- points: bfloat16 [1024, 768], P(('groups', 'cent')), parts along dimension 0, may hold values from -64 to 64, as said below
- centroids: bfloat16 [131072, 768], P(('groups', 'cent')), parts along dimension 0, may hold values from -1 to 1
- coarse_init: float32 [4096, 768], P(('groups', 'cent')), parts along dimension 0, may hold values from -2.4 to 2.4
- assign: int32 [131072], P(('groups', 'cent')), parts along dimension 0, may hold values from 0 to 2047, as said below
Outputs:
- level_one: bfloat16 [131072, 768], P(('groups', 'cent')), parts along dimension 0
- level_two: float32 [4096, 768], P(('groups', 'cent')), parts along dimension 0
The draws below stay inside these ranges and needn't reach their ends.
There are 2 independent parts, one for each index of `groups`. The reference program is written for one: setup_inputs(seed, part) draws one part's arguments, and reference() takes and returns one part's arrays. A program takes and returns all parts, laid end to end along the dimension named above; each array names one. Nothing has to cross between parts.
Inputs may be any that keep to these rules, and one draw needn't show every extreme that they name: `points`: entries normal (clipped at 8) or uniform within 1.7; on some draws a few rows are scaled multiples of a centroid that has a close twin, giving logits up to about 300. `assign`: among the 65536 // 16 level-1 centroids held by one index of cent, at most 512 have their level-2 centroid in any one block of 2048 // 16 consecutive level-2 centroids, and some block receives exactly 512.
All inputs are finite; a program needn't handle non-finite values.
Results may differ from the reference program's by a relative error of at most 0.0039.
Values may be sent and summed in bfloat16 or wider, within the bound.
No kernel may reach another device: no remote copies, remote signals or barrier semaphores. Data moves between devices by JAX's collectives and lax.ppermute only.
A program may use at most 64 MiB of HBM per device.

```python
import math
import jax
import jax.numpy as jnp
from jax import lax

D = 768
K1 = 65536
K2 = 2048
PTS = 512
CAP = 512
N_CENT = 16


def pair_draw(key):
    key_pts, key_cen = jax.random.split(jax.random.fold_in(key, 7), 2)
    points = jnp.clip(jax.random.normal(key_pts, (PTS, D), jnp.float32), -8.0, 8.0)
    cents = jnp.clip(0.1 * jax.random.normal(key_cen, (K1, D), jnp.float32), -0.8, 0.8)
    return (points, cents)


def draw_points(key, part):
    return pair_draw(key)[0].astype(jnp.bfloat16)


def draw_centroids(key, part):
    return pair_draw(key)[1].astype(jnp.bfloat16)


def draw_assign(key, part):
    local = K1 // N_CENT
    own = K2 // N_CENT
    limit = CAP

    def one_block(block_key):
        key_perm, key_mix, key_inner = jax.random.split(block_key, 3)
        owners = jax.random.permutation(key_perm, N_CENT)
        dest = owners[jnp.arange(local, dtype=jnp.int32) // limit]
        dest = jax.random.permutation(key_mix, dest)
        inner = jax.random.randint(key_inner, (local,), 0, own, jnp.int32)
        return dest.astype(jnp.int32) * own + inner
    keys = jax.random.split(jax.random.fold_in(key, 11), N_CENT)
    return jax.vmap(one_block)(keys).reshape(K1).astype(jnp.int32)


def level_of(stream_key, extent, pieces, least, top_value):
    def one(axis_at, blocks):
        steps = jax.random.uniform(jax.random.fold_in(jax.random.fold_in(stream_key, 6), axis_at), (blocks,), jnp.float32, least / len(pieces), top_value / len(pieces))
        return jnp.repeat(jnp.exp(steps), extent[axis_at] // blocks).reshape((-1,) + (1,) * (len(extent) - axis_at - 1))

    gain = one(*pieces[0])
    for cut in pieces[1:]:
        gain = gain * one(*cut)
    return gain


def bell_draw(key, shape, spread, most, cuts=(), kind=jnp.bfloat16):
    drawn = jax.random.normal(key, shape, jnp.float32) * spread
    if len(cuts) > 0:
        drawn = level_of(key, shape, cuts, -0.22, 0.18) * drawn
    return jnp.clip(drawn, min=-most, max=most).astype(kind)


def setup_inputs(seed: int = 0, part: int = 0) -> dict:
    key_of = jax.random.split(jax.random.key(seed), 5)
    part_splits = jax.random.split(jax.random.fold_in(key_of[4], part), 5)
    points = draw_points(jax.random.fold_in(jax.random.fold_in(key_of[4], part), 71), part)
    centroids = draw_centroids(jax.random.fold_in(jax.random.fold_in(key_of[4], part), 71), part)
    coarse_init = bell_draw(part_splits[2], (K2, D), 0.3, 2.4, ((0, 16),), jnp.float32)
    assign = draw_assign(jax.random.fold_in(jax.random.fold_in(key_of[4], part), 71), part)
    return dict(points=points, centroids=centroids, coarse_init=coarse_init, assign=assign)


TEMP = 0.05
PRIOR_ONE = 0.02
PRIOR_TWO = 0.25

def reference(points, centroids, coarse_init, assign):
    scale = 1.0 / (TEMP * math.sqrt(D))
    width = min(4096, K1)
    cblocks = centroids.reshape(K1 // width, width, D)

    def logits_of(block):
        return jnp.dot(points, block.T, preferred_element_type=jnp.float32) * scale

    def top_step(carry, block):
        return (jnp.maximum(carry, lax.optimization_barrier(jnp.max(logits_of(block), axis=1))), None)
    peak, _ = lax.scan(top_step, jnp.full((PTS,), -jnp.inf, jnp.float32), cblocks)

    def sum_step(carry, block):
        return (carry + lax.optimization_barrier(jnp.sum(jnp.exp(logits_of(block) - peak[:, None]), axis=1)), None)
    total, _ = lax.scan(sum_step, jnp.zeros((PTS,), jnp.float32), cblocks)

    def update(block):
        resp = jnp.exp(logits_of(block) - peak[:, None]) / total[:, None]
        mass = lax.optimization_barrier(jnp.sum(resp, axis=0))
        weighted = jnp.dot(resp.astype(jnp.bfloat16).T, points, preferred_element_type=jnp.float32)
        fresh = (weighted + PRIOR_ONE * block.astype(jnp.float32)) / (mass[:, None] + PRIOR_ONE)
        return (fresh, mass)
    fresh, mass = lax.map(update, cblocks)
    fresh = fresh.reshape(K1, D)
    mass = mass.reshape(K1)
    level_one = fresh.astype(jnp.bfloat16)
    moved = (mass[:, None] * fresh).astype(jnp.bfloat16)
    wsum = jax.ops.segment_sum(moved.astype(jnp.float32), assign, K2)
    msum = jax.ops.segment_sum(mass, assign, K2)
    level_two = (wsum + PRIOR_TWO * coarse_init) / (msum[:, None] + PRIOR_TWO)
    return (level_one, level_two)
```

```python
import functools
import math

import jax
import jax.numpy as jnp
from jax import lax
from jax.experimental import pallas as pl
from jax.experimental.pallas import tpu as pltpu
from jax.sharding import PartitionSpec as P

TEMP = 0.05
PRIOR_ONE = 0.02
PRIOR_TWO = 0.25
TILES = 8
LANES = 128
SUB = 8
F32 = jnp.float32
BF16 = jnp.bfloat16
VMEM_LIMIT = 48 << 20


def exchange(value, mask, n):
    return lax.ppermute(value, "cent", [(i, i ^ mask) for i in range(n)])


def full(shape):
    return pl.BlockSpec(shape, lambda *_: (0,) * len(shape))


def whole():
    return pl.BlockSpec(memory_space=pltpu.VMEM)


def logits_kernel(n, kappa, own_ref, far_ref, cen_ref, x_ref, e_ref, m_ref, st_ref, s_ref):
    t = pl.program_id(0)
    rows = x_ref.shape[0] // n

    @pl.when(t == 0)
    def _():
        me = lax.axis_index("cent")
        for m in range(n // 2):
            for ref, low in ((own_ref, 0), (far_ref, 1)):
                at = pl.multiple_of((me ^ (2 * m + low)) * rows, rows)
                x_ref[pl.ds(at, rows), :] = ref[pl.ds(m * rows, rows), :]

    logits = lax.dot_general(
        cen_ref[...], x_ref[...], (((1,), (1,)), ((), ())), preferred_element_type=F32
    )
    top = jnp.max(logits, axis=0, keepdims=True)
    e = jnp.exp2((logits - top) * kappa)
    e_ref[...] = e.astype(BF16)
    m_ref[pl.ds(t, 1), :] = top
    s_ref[pl.ds(t, 1), :] = jnp.sum(e, axis=0, keepdims=True)

    @pl.when(t == pl.num_programs(0) - 1)
    def _():
        best = jnp.max(m_ref[...], axis=0, keepdims=True)
        st_ref[0:1, :] = best
        st_ref[1:2, :] = jnp.sum(
            s_ref[...] * jnp.exp2((m_ref[...] - best) * kappa), axis=0, keepdims=True
        )


def logits_call(n, kappa, own, far, centroids):
    local_k, width = centroids.shape
    points = 2 * own.shape[0]
    tk = local_k // TILES
    return pl.pallas_call(
        functools.partial(logits_kernel, n, kappa),
        grid=(TILES,),
        in_specs=[
            full(own.shape),
            full(far.shape),
            pl.BlockSpec((tk, width), lambda t: (t, 0)),
        ],
        out_specs=[
            full((points, width)),
            pl.BlockSpec((tk, points), lambda t: (t, 0)),
            full((TILES, points)),
            full((2, points)),
        ],
        out_shape=[
            jax.ShapeDtypeStruct((points, width), BF16),
            jax.ShapeDtypeStruct((local_k, points), BF16),
            jax.ShapeDtypeStruct((TILES, points), F32),
            jax.ShapeDtypeStruct((2, points), F32),
        ],
        scratch_shapes=[pltpu.VMEM((TILES, points), F32)],
        compiler_params=pltpu.CompilerParams(vmem_limit_bytes=VMEM_LIMIT),
        name="logits",
    )(own, far, centroids)


def mass_rows(column_masses):
    eye = lax.broadcasted_iota(jnp.int32, column_masses.shape, 0) == lax.broadcasted_iota(
        jnp.int32, column_masses.shape, 1
    )
    return jnp.sum(jnp.where(eye, column_masses, 0.0), axis=0, keepdims=True)


def pack_mass(row, width):
    high = row.astype(BF16).astype(F32)
    low = row - high
    pad = jnp.zeros((1, width - 2 * LANES), F32)
    line = jnp.concatenate([high, low, pad], axis=1)
    return jnp.broadcast_to(line, (SUB, width)).astype(BF16)


def unpack_mass(rows):
    line = rows[0:1, :].astype(F32)
    return line[:, :LANES] + line[:, LANES : 2 * LANES]


def update_kernel(
    n, kappa, r1, asg_ref, e_ref, cen_ref, x_ref, m_ref, st_ref,
    one_ref, send_ref, keep_ref, mv_ref, acc_ref,
):
    t = pl.program_id(0)
    tk, width = cen_ref.shape
    chunks = width // LANES
    k2 = acc_ref.shape[0] // SUB - 1

    @pl.when(t == 0)
    def _():
        step = 16 * SUB

        def clear(i, _):
            acc_ref[pl.ds(pl.multiple_of(i * step, step), step), :] = jnp.zeros((step, LANES), F32)
            return _

        lax.fori_loop(0, k2 * SUB // step, clear, 0)

    factor = jnp.exp2((m_ref[pl.ds(t, 1), :] - st_ref[0:1, :]) * kappa) / st_ref[1:2, :]
    resp = e_ref[...].astype(F32) * factor
    mass = jnp.sum(resp, axis=1, keepdims=True)
    weighted = jnp.dot(resp.astype(BF16), x_ref[...], preferred_element_type=F32)
    fresh = (weighted + PRIOR_ONE * cen_ref[...].astype(F32)) * (1.0 / (mass + PRIOR_ONE))
    one_ref[...] = fresh.astype(BF16)
    moved = (mass * fresh).astype(BF16).astype(F32)
    for d in range(chunks):
        mv_ref[pl.ds(d, tk, stride=SUB), :] = moved[:, d * LANES : (d + 1) * LANES]
    mv_ref[pl.ds(chunks, tk, stride=SUB), :] = jnp.broadcast_to(mass, (tk, LANES))

    unroll = 8

    def scatter(i, _):
        for u in range(unroll):
            k = i * unroll + u
            to = pl.ds(pl.multiple_of(asg_ref[t * tk + k] * SUB, SUB), SUB)
            acc_ref[to, :] = acc_ref[to, :] + mv_ref[pl.ds(pl.multiple_of(k * SUB, SUB), SUB), :]
        return _

    lax.fori_loop(0, tk // unroll, scatter, 0)

    @pl.when(t == pl.num_programs(0) - 1)
    def _():
        me = lax.axis_index("cent")
        rows = k2 // n
        half = n // 2
        r2 = rows - r1
        later = half * r1
        for u in range(half):
            first = (1 - u % 2) * (half // 2) + u // 2
            for ref, low in ((send_ref, 1), (keep_ref, 0)):
                base = pl.multiple_of((me ^ (2 * u + low)) * (rows * SUB), SUB)
                at2 = later + u * (r2 + SUB)
                for d in range(chunks):
                    col = slice(d * LANES, (d + 1) * LANES)
                    part = acc_ref[pl.ds(base + d, rows, stride=SUB), :].astype(BF16)
                    ref[first * r1 : (first + 1) * r1, col] = part[:r1]
                    ref[at2 : at2 + r2, col] = part[r1:]
                row = mass_rows(acc_ref[pl.ds(base + chunks, rows, stride=SUB), :])
                ref[at2 + r2 : at2 + r2 + SUB, :] = pack_mass(row, width)


def update_call(n, kappa, k2, r1, assign, e, centroids, x, m, stats):
    local_k, width = centroids.shape
    points = x.shape[0]
    tk = local_k // TILES
    message = (n // 2) * (k2 // n + SUB)
    return pl.pallas_call(
        functools.partial(update_kernel, n, kappa, r1),
        grid=(TILES,),
        in_specs=[
            pl.BlockSpec(memory_space=pltpu.SMEM),
            pl.BlockSpec((tk, points), lambda t: (t, 0)),
            pl.BlockSpec((tk, width), lambda t: (t, 0)),
            full(x.shape),
            full(m.shape),
            full(stats.shape),
        ],
        out_specs=[
            pl.BlockSpec((tk, width), lambda t: (t, 0)),
            full((message, width)),
            full((message, width)),
        ],
        out_shape=[
            jax.ShapeDtypeStruct((local_k, width), BF16),
            jax.ShapeDtypeStruct((message, width), BF16),
            jax.ShapeDtypeStruct((message, width), BF16),
        ],
        scratch_shapes=[
            pltpu.VMEM(((tk + 1) * SUB, LANES), F32),
            pltpu.VMEM(((k2 + 1) * SUB, LANES), F32),
        ],
        compiler_params=pltpu.CompilerParams(vmem_limit_bytes=VMEM_LIMIT),
        name="update",
    )(assign, e, centroids, x, m, stats)


def add_rows(parts, rows):
    total = parts[0][rows, :].astype(F32)
    for ref in parts[1:]:
        total = total + ref[rows, :].astype(F32)
    return total


def add_mass(parts, rows):
    total = unpack_mass(parts[0][rows, :])
    for ref in parts[1:]:
        total = total + unpack_mass(ref[rows, :])
    return total


def sum1_kernel(half, r1, r2, keep_ref, got_ref, ysend_ref, ykeep_ref, zkeep_ref, *zsend_refs):
    quarter = half // 2
    both = (keep_ref, got_ref)
    for b in range(half):
        ref, at = (ysend_ref, b) if b < quarter else (ykeep_ref, b - quarter)
        ref[at * r1 : (at + 1) * r1, :] = add_rows(both, slice(b * r1, (b + 1) * r1)).astype(BF16)
    size = r2 + SUB
    for b in range(half):
        ref = (zkeep_ref, *zsend_refs)[b // 2]
        at = (b % 2) * size
        src = half * r1 + b * size
        ref[at : at + r2, :] = add_rows(both, slice(src, src + r2)).astype(BF16)
        mass = add_mass(both, slice(src + r2, src + size))
        ref[at + r2 : at + size, :] = pack_mass(mass, ref.shape[1])


def sum2_kernel(quarter, r1, r2, *refs):
    ykeep_ref, ygot_ref, zkeep_ref = refs[:3]
    zgot = refs[3 : 2 + quarter]
    outs = refs[2 + quarter :]
    hkeep_ref, tkeep_ref, tsend_ref = outs[:3]
    hsend = outs[3:]
    for b in range(quarter):
        ref = (hkeep_ref, *hsend)[b]
        ref[...] = add_rows((ykeep_ref, ygot_ref), slice(b * r1, (b + 1) * r1)).astype(BF16)
    parts = (zkeep_ref, *zgot)
    size = r2 + SUB
    for y, ref in ((0, tkeep_ref), (1, tsend_ref)):
        src = y * size
        ref[0:r2, :] = add_rows(parts, slice(src, src + r2)).astype(BF16)
        mass = add_mass(parts, slice(src + r2, src + size))
        ref[r2:size, :] = pack_mass(mass, ref.shape[1])


def sum3_kernel(quarter, r1, r2, *refs):
    coarse_ref = refs[0]
    head = refs[1 : 1 + quarter]
    tail = refs[1 + quarter : 3 + quarter]
    out_ref = refs[-1]
    rows = r1 + r2
    mass = add_mass(tail, slice(r2, r2 + SUB))
    shape = (rows, LANES)
    eye = lax.broadcasted_iota(jnp.int32, shape, 0) == lax.broadcasted_iota(jnp.int32, shape, 1)
    column = jnp.sum(jnp.where(eye, mass, 0.0), axis=1, keepdims=True)
    inverse = 1.0 / (column + PRIOR_TWO)
    first = add_rows(head, slice(0, r1)) + PRIOR_TWO * coarse_ref[0:r1, :]
    out_ref[0:r1, :] = first * inverse[0:r1]
    second = add_rows(tail, slice(0, r2)) + PRIOR_TWO * coarse_ref[r1:rows, :]
    out_ref[r1:rows, :] = second * inverse[r1:rows]


def simple_call(kernel, name, shapes, dtype, *args):
    out = pl.pallas_call(
        kernel,
        in_specs=[whole() for _ in args],
        out_specs=[whole() for _ in shapes],
        out_shape=[jax.ShapeDtypeStruct(s, dtype) for s in shapes],
        compiler_params=pltpu.CompilerParams(vmem_limit_bytes=32 << 20),
        name=name,
    )(*args)
    return out


def shards(n, points, centroids, coarse_init, assign):
    width = points.shape[1]
    rows = coarse_init.shape[0]
    k2 = rows * n
    kappa = math.log2(math.e) / (TEMP * math.sqrt(width))
    steps = range(1, n // 4)

    b = jnp.concatenate([points] + [exchange(points, 4 * s, n) for s in steps])
    b = b.reshape(n // 4, 1, *points.shape)
    b = jnp.concatenate([b, exchange(b, 2, n)], axis=1).reshape(-1, width)
    far = exchange(b, 1, n)

    x, e, m, stats = logits_call(n, kappa, b, far, centroids)

    bit = 1
    while bit < n:
        other = exchange(stats, bit, n)
        top = jnp.maximum(stats[0], other[0])
        total = stats[1] * jnp.exp2((stats[0] - top) * kappa) + other[1] * jnp.exp2(
            (other[0] - top) * kappa
        )
        stats = jnp.stack([top, total])
        bit *= 2

    r1 = max(16, (rows * 5 // 8) // 16 * 16)
    r2 = rows - r1
    level_one, send, keep = update_call(
        n, kappa, k2, r1, assign, e, centroids, x, m, stats
    )

    half, quarter = n // 2, n // 4
    got = exchange(send, 1, n)
    size = r2 + SUB
    ysend, ykeep, zkeep, *zsend = simple_call(
        functools.partial(sum1_kernel, half, r1, r2), "sum1",
        [(quarter * r1, width)] * 2 + [(2 * size, width)] * quarter, BF16, keep, got,
    )
    ygot = exchange(ysend, 2, n)
    zgot = [exchange(v, 4 * (s + 1), n) for s, v in enumerate(zsend)]
    hkeep, tkeep, tsend, *hsend = simple_call(
        functools.partial(sum2_kernel, quarter, r1, r2), "sum2",
        [(r1, width)] + [(size, width)] * 2 + [(r1, width)] * (quarter - 1), BF16,
        ykeep, ygot, zkeep, *zgot,
    )
    hgot = [exchange(v, 4 * (s + 1), n) for s, v in enumerate(hsend)]
    tgot = exchange(tsend, 2, n)
    (level_two,) = simple_call(
        functools.partial(sum3_kernel, quarter, r1, r2), "sum3",
        [(rows, width)], F32, coarse_init, hkeep, *hgot, tkeep, tgot,
    )
    return (level_one, level_two)


def solution(mesh):
    n = mesh.shape["cent"]
    both = ("groups", "cent")
    return jax.shard_map(
        functools.partial(shards, n),
        mesh=mesh,
        in_specs=(P(both, None), P(both, None), P(both, None), P(both)),
        out_specs=(P(both, None), P(both, None)),
        check_vma=False,
    )
```

```python
import functools
import math

import jax
import jax.numpy as jnp
from jax import lax
from jax.experimental import pallas as pl
from jax.experimental.pallas import tpu as pltpu
from jax.sharding import PartitionSpec as P

TEMP = 0.05
PRIOR_ONE = 0.02
PRIOR_TWO = 0.25
TILES = 8
ACCS = 2
LANES = 128
SUB = 8
F32 = jnp.float32
BF16 = jnp.bfloat16


def exchange(value, mask, n):
    return lax.ppermute(value, "cent", [(i, i ^ mask) for i in range(n)])


def whole():
    return pl.BlockSpec(memory_space=pltpu.VMEM)


def logits_kernel(n, kappa, own_ref, far_ref, cen_ref, x_ref, e_ref, m_ref, st_ref, s_ref):
    t = pl.program_id(0)
    rows = x_ref.shape[0] // n

    @pl.when(t == 0)
    def _():
        me = lax.axis_index("cent")
        for m in range(n // 2):
            for ref, low in ((own_ref, 0), (far_ref, 1)):
                at = pl.multiple_of((me ^ (2 * m + low)) * rows, rows)
                x_ref[pl.ds(at, rows), :] = ref[pl.ds(m * rows, rows), :]

    tk = cen_ref.shape[0] // TILES
    here = pl.ds(pl.multiple_of(t * tk, tk), tk)
    logits = lax.dot_general(
        cen_ref[here, :], x_ref[...], (((1,), (1,)), ((), ())), preferred_element_type=F32
    )
    top = jnp.max(logits, axis=0, keepdims=True)
    e = jnp.exp2((logits - top) * kappa)
    e_ref[here, :] = e.astype(BF16)
    m_ref[pl.ds(t, 1), :] = top
    s_ref[pl.ds(t, 1), :] = jnp.sum(e, axis=0, keepdims=True)

    @pl.when(t == pl.num_programs(0) - 1)
    def _():
        best = jnp.max(m_ref[...], axis=0, keepdims=True)
        st_ref[0:1, :] = best
        st_ref[1:2, :] = jnp.sum(
            s_ref[...] * jnp.exp2((m_ref[...] - best) * kappa), axis=0, keepdims=True
        )


def logits_call(n, kappa, own, far, centroids):
    local_k, width = centroids.shape
    points = 2 * own.shape[0]
    return pl.pallas_call(
        functools.partial(logits_kernel, n, kappa),
        grid=(TILES,),
        in_specs=[whole()] * 3,
        out_specs=[whole()] * 4,
        out_shape=[
            jax.ShapeDtypeStruct((points, width), BF16),
            jax.ShapeDtypeStruct((local_k, points), BF16),
            jax.ShapeDtypeStruct((TILES, points), F32),
            jax.ShapeDtypeStruct((2, points), F32),
        ],
        scratch_shapes=[pltpu.VMEM((TILES, points), F32)],
        compiler_params=pltpu.CompilerParams(vmem_limit_bytes=16 << 20),
        name="logits",
    )(own, far, centroids)


def fetch_kernel(cen_ref, out_ref, sem):
    copy = pltpu.make_async_copy(cen_ref, out_ref, sem)
    copy.start()
    copy.wait()


def fetch_call(centroids):
    return pl.pallas_call(
        fetch_kernel,
        in_specs=[pl.BlockSpec(memory_space=pltpu.HBM)],
        out_specs=whole(),
        out_shape=jax.ShapeDtypeStruct(centroids.shape, centroids.dtype),
        scratch_shapes=[pltpu.SemaphoreType.DMA],
        cost_estimate=pl.CostEstimate(
            flops=0, bytes_accessed=2 * centroids.size * 2, transcendentals=0
        ),
        compiler_params=pltpu.CompilerParams(vmem_limit_bytes=8 << 20),
        name="fetch",
    )(centroids)


def mass_rows(column_masses):
    eye = lax.broadcasted_iota(jnp.int32, column_masses.shape, 0) == lax.broadcasted_iota(
        jnp.int32, column_masses.shape, 1
    )
    return jnp.sum(jnp.where(eye, column_masses, 0.0), axis=0, keepdims=True)


def pack_mass(row, width):
    high = row.astype(BF16).astype(F32)
    low = row - high
    pad = jnp.zeros((1, width - 2 * LANES), F32)
    line = jnp.concatenate([high, low, pad], axis=1)
    return jnp.broadcast_to(line, (SUB, width)).astype(BF16)


def unpack_mass(rows):
    line = rows[0:1, :].astype(F32)
    return line[:, :LANES] + line[:, LANES : 2 * LANES]


def update_kernel(
    n, kappa, r1, asg_ref, dup_ref, e_ref, cen_ref, x_ref, m_ref, st_ref,
    one_ref, send_ref, keep_ref, mv_ref, *accs,
):
    t = pl.program_id(0)
    width = cen_ref.shape[1]
    tk = one_ref.shape[0]
    chunks = width // LANES
    k2 = accs[0].shape[0] // SUB - SUB

    @pl.when(t == 0)
    def _():
        for ref in (*accs, mv_ref):
            step = 8 * SUB

            def clear(i, _):
                ref[pl.ds(pl.multiple_of(i * step, step), step), :] = jnp.zeros((step, LANES), F32)
                return _

            lax.fori_loop(0, ref.shape[0] // step, clear, 0)

    def scatter(offsets, dups, rows):
        news = []
        for i, row in enumerate(rows):
            at = pl.ds(pl.multiple_of(offsets[i], SUB), SUB)
            if i >= ACCS:
                row = row + rows[i - ACCS] * dups[i - ACCS]
            news.append((accs[i % ACCS], at, accs[i % ACCS][at, :] + row))
        for ref, at, new in news:
            ref[at, :] = new

    before = pl.ds(pl.multiple_of(jnp.maximum(t - 1, 0) * tk, tk), tk)
    asg_view, dup_view = asg_ref.at[before], dup_ref.at[before]
    for k in range(0, tk, 2 * ACCS):
        group = range(k, k + 2 * ACCS)
        scatter(
            [asg_view[i] for i in group],
            [dup_view[i] for i in group[:ACCS]],
            [mv_ref[i * SUB : (i + 1) * SUB, :] for i in group],
        )

    here = pl.ds(pl.multiple_of(t * tk, tk), tk)
    factor = jnp.exp2((m_ref[pl.ds(t, 1), :] - st_ref[0:1, :]) * kappa) / st_ref[1:2, :]
    resp = e_ref[here, :].astype(F32) * factor
    mass = jnp.sum(resp, axis=1, keepdims=True)
    weighted = jnp.dot(resp.astype(BF16), x_ref[...], preferred_element_type=F32)
    fresh = (weighted + PRIOR_ONE * cen_ref[here, :].astype(F32)) * (1.0 / (mass + PRIOR_ONE))
    one_ref[...] = fresh.astype(BF16)
    moved = (mass * fresh).astype(BF16).astype(F32)
    for d in range(chunks):
        mv_ref[pl.ds(d, tk, stride=SUB), :] = moved[:, d * LANES : (d + 1) * LANES]
    mv_ref[pl.ds(chunks, tk, stride=SUB), :] = jnp.broadcast_to(mass, (tk, LANES))

    @pl.when(t == pl.num_programs(0) - 1)
    def _():
        unroll = 32

        def last(i, _):
            for u in range(0, unroll, 2 * ACCS):
                group = range(u, u + 2 * ACCS)
                base = t * tk + i * unroll
                scatter(
                    [asg_ref[base + v] for v in group],
                    [dup_ref[base + v] for v in group[:ACCS]],
                    [
                        mv_ref[pl.ds(pl.multiple_of((i * unroll + v) * SUB, SUB), SUB), :]
                        for v in group
                    ],
                )
            return _

        lax.fori_loop(0, tk // unroll, last, 0)
        step = 8 * SUB

        def merge(i, _):
            at = pl.ds(pl.multiple_of(i * step, step), step)
            total = accs[0][at, :]
            for ref in accs[1:]:
                total = total + ref[at, :]
            accs[0][at, :] = total
            return _

        if ACCS > 1:
            lax.fori_loop(0, k2 * SUB // step, merge, 0)
        acc_ref = accs[0]
        me = lax.axis_index("cent")
        rows = k2 // n
        half = n // 2
        r2 = rows - r1
        later = half * r1
        for u in range(half):
            first = (1 - u % 2) * (half // 2) + u // 2
            for ref, low in ((send_ref, 1), (keep_ref, 0)):
                base = pl.multiple_of((me ^ (2 * u + low)) * (rows * SUB), SUB)
                at2 = later + u * (r2 + SUB)
                for d in range(chunks):
                    col = slice(d * LANES, (d + 1) * LANES)
                    part = acc_ref[pl.ds(base + d, rows, stride=SUB), :].astype(BF16)
                    ref[first * r1 : (first + 1) * r1, col] = part[:r1]
                    ref[at2 : at2 + r2, col] = part[r1:]
                row = mass_rows(acc_ref[pl.ds(base + chunks, rows, stride=SUB), :])
                ref[at2 + r2 : at2 + r2 + SUB, :] = pack_mass(row, width)


def update_call(n, kappa, k2, r1, assign, e, centroids, x, m, stats):
    local_k, width = centroids.shape
    tk = local_k // TILES
    message = (n // 2) * (k2 // n + SUB)
    return pl.pallas_call(
        functools.partial(update_kernel, n, kappa, r1),
        grid=(TILES,),
        in_specs=[
            *[pl.BlockSpec(memory_space=pltpu.SMEM)] * 2,
            *[whole()] * 5,
        ],
        out_specs=[pl.BlockSpec((tk, width), lambda t: (t, 0)), whole(), whole()],
        out_shape=[
            jax.ShapeDtypeStruct((local_k, width), BF16),
            jax.ShapeDtypeStruct((message, width), BF16),
            jax.ShapeDtypeStruct((message, width), BF16),
        ],
        scratch_shapes=[
            pltpu.VMEM(((tk + SUB) * SUB, LANES), F32),
            *[pltpu.VMEM(((k2 + SUB) * SUB, LANES), F32)] * ACCS,
        ],
        compiler_params=pltpu.CompilerParams(vmem_limit_bytes=34 << 20),
        name="update",
    )(assign * SUB, (assign == jnp.roll(assign, -ACCS)).astype(F32), e, centroids, x, m, stats)


def add_rows(parts, rows):
    total = parts[0][rows, :].astype(F32)
    for ref in parts[1:]:
        total = total + ref[rows, :].astype(F32)
    return total


def add_mass(parts, rows):
    total = unpack_mass(parts[0][rows, :])
    for ref in parts[1:]:
        total = total + unpack_mass(ref[rows, :])
    return total


def sum1_kernel(half, r1, r2, keep_ref, got_ref, ysend_ref, ykeep_ref, zkeep_ref, *zsend_refs):
    quarter = half // 2
    both = (keep_ref, got_ref)
    for b in range(half):
        ref, at = (ysend_ref, b) if b < quarter else (ykeep_ref, b - quarter)
        ref[at * r1 : (at + 1) * r1, :] = add_rows(both, slice(b * r1, (b + 1) * r1)).astype(BF16)
    size = r2 + SUB
    for b in range(half):
        ref = (zkeep_ref, *zsend_refs)[b // 2]
        at = (b % 2) * size
        src = half * r1 + b * size
        ref[at : at + r2, :] = add_rows(both, slice(src, src + r2)).astype(BF16)
        mass = add_mass(both, slice(src + r2, src + size))
        ref[at + r2 : at + size, :] = pack_mass(mass, ref.shape[1])


def sum2_kernel(quarter, r1, r2, *refs):
    ykeep_ref, ygot_ref, zkeep_ref = refs[:3]
    zgot = refs[3 : 2 + quarter]
    outs = refs[2 + quarter :]
    hkeep_ref, tkeep_ref, tsend_ref = outs[:3]
    hsend = outs[3:]
    for b in range(quarter):
        ref = (hkeep_ref, *hsend)[b]
        ref[...] = add_rows((ykeep_ref, ygot_ref), slice(b * r1, (b + 1) * r1)).astype(BF16)
    parts = (zkeep_ref, *zgot)
    size = r2 + SUB
    for y, ref in ((0, tkeep_ref), (1, tsend_ref)):
        src = y * size
        ref[0:r2, :] = add_rows(parts, slice(src, src + r2)).astype(BF16)
        mass = add_mass(parts, slice(src + r2, src + size))
        ref[r2:size, :] = pack_mass(mass, ref.shape[1])


def sum3_kernel(quarter, r1, r2, *refs):
    coarse_ref = refs[0]
    head = refs[1 : 1 + quarter]
    tail = refs[1 + quarter : 3 + quarter]
    out_ref = refs[-1]
    rows = r1 + r2
    mass = add_mass(tail, slice(r2, r2 + SUB))
    shape = (rows, LANES)
    eye = lax.broadcasted_iota(jnp.int32, shape, 0) == lax.broadcasted_iota(jnp.int32, shape, 1)
    column = jnp.sum(jnp.where(eye, mass, 0.0), axis=1, keepdims=True)
    inverse = 1.0 / (column + PRIOR_TWO)
    first = add_rows(head, slice(0, r1)) + PRIOR_TWO * coarse_ref[0:r1, :]
    out_ref[0:r1, :] = first * inverse[0:r1]
    second = add_rows(tail, slice(0, r2)) + PRIOR_TWO * coarse_ref[r1:rows, :]
    out_ref[r1:rows, :] = second * inverse[r1:rows]


def simple_call(kernel, name, shapes, dtype, *args):
    out = pl.pallas_call(
        kernel,
        in_specs=[whole() for _ in args],
        out_specs=[whole() for _ in shapes],
        out_shape=[jax.ShapeDtypeStruct(s, dtype) for s in shapes],
        compiler_params=pltpu.CompilerParams(vmem_limit_bytes=32 << 20),
        name=name,
    )(*args)
    return out


def shards(n, points, centroids, coarse_init, assign):
    width = points.shape[1]
    rows = coarse_init.shape[0]
    k2 = rows * n
    kappa = math.log2(math.e) / (TEMP * math.sqrt(width))
    steps = range(1, n // 4)

    b = jnp.concatenate([points] + [exchange(points, 4 * s, n) for s in steps])
    b, centroids = lax.optimization_barrier((b, fetch_call(centroids)))
    b = b.reshape(n // 4, 1, *points.shape)
    b = jnp.concatenate([b, exchange(b, 2, n)], axis=1).reshape(-1, width)
    far = exchange(b, 1, n)

    x, e, m, stats = logits_call(n, kappa, b, far, centroids)

    bit = 1
    while bit < n:
        other = exchange(stats, bit, n)
        top = jnp.maximum(stats[0], other[0])
        total = stats[1] * jnp.exp2((stats[0] - top) * kappa) + other[1] * jnp.exp2(
            (other[0] - top) * kappa
        )
        stats = jnp.stack([top, total])
        bit *= 2

    r1 = max(16, (rows * 5 // 8) // 16 * 16)
    r2 = rows - r1
    level_one, send, keep = update_call(
        n, kappa, k2, r1, assign, e, centroids, x, m, stats
    )

    half, quarter = n // 2, n // 4
    got = exchange(send, 1, n)
    size = r2 + SUB
    ysend, ykeep, zkeep, *zsend = simple_call(
        functools.partial(sum1_kernel, half, r1, r2), "sum1",
        [(quarter * r1, width)] * 2 + [(2 * size, width)] * quarter, BF16, keep, got,
    )
    ygot = exchange(ysend, 2, n)
    zgot = [exchange(v, 4 * (s + 1), n) for s, v in enumerate(zsend)]
    hkeep, tkeep, tsend, *hsend = simple_call(
        functools.partial(sum2_kernel, quarter, r1, r2), "sum2",
        [(r1, width)] + [(size, width)] * 2 + [(r1, width)] * (quarter - 1), BF16,
        ykeep, ygot, zkeep, *zgot,
    )
    hgot = [exchange(v, 4 * (s + 1), n) for s, v in enumerate(hsend)]
    tgot = exchange(tsend, 2, n)
    (level_two,) = simple_call(
        functools.partial(sum3_kernel, quarter, r1, r2), "sum3",
        [(rows, width)], F32, coarse_init, hkeep, *hgot, tkeep, tgot,
    )
    return (level_one, level_two)


def solution(mesh):
    n = mesh.shape["cent"]
    both = ("groups", "cent")
    return jax.shard_map(
        functools.partial(shards, n),
        mesh=mesh,
        in_specs=(P(both, None), P(both, None), P(both, None), P(both)),
        out_specs=(P(both, None), P(both, None)),
        check_vma=False,
    )
```

```python
import functools
import math

import jax
import jax.numpy as jnp
from jax import lax
from jax.experimental import pallas as pl
from jax.experimental.pallas import tpu as pltpu
from jax.sharding import PartitionSpec as P

TEMP = 0.05
PRIOR_ONE = 0.02
PRIOR_TWO = 0.25
TILES = 8
ACCS = 2
LANES = 128
SUB = 8
F32 = jnp.float32
BF16 = jnp.bfloat16


def exchange(value, mask, n):
    return lax.ppermute(value, "cent", [(i, i ^ mask) for i in range(n)])


def powers(low, high):
    return [low << i for i in range(high.bit_length()) if low << i < high]


def whole():
    return pl.BlockSpec(memory_space=pltpu.VMEM)


def logits_kernel(n, kappa, masks, own_ref, far_ref, cen_ref, x_ref, e_ref, m_ref, st_ref, s_ref):
    t = pl.program_id(0)
    rows = x_ref.shape[0] // n

    @pl.when(t == 0)
    def _():
        me = lax.axis_index("cent")
        for i, mask in enumerate(masks):
            for ref, low in ((own_ref, 0), (far_ref, 1)):
                at = pl.multiple_of((me ^ mask ^ low) * rows, rows)
                x_ref[pl.ds(at, rows), :] = ref[pl.ds(i * rows, rows), :]

    tk = cen_ref.shape[0] // TILES
    here = pl.ds(pl.multiple_of(t * tk, tk), tk)
    logits = lax.dot_general(
        cen_ref[here, :], x_ref[...], (((1,), (1,)), ((), ())), preferred_element_type=F32
    )
    top = jnp.max(logits, axis=0, keepdims=True)
    e = jnp.exp2((logits - top) * kappa)
    e_ref[here, :] = e.astype(BF16)
    m_ref[pl.ds(t, 1), :] = top
    s_ref[pl.ds(t, 1), :] = jnp.sum(e, axis=0, keepdims=True)

    @pl.when(t == pl.num_programs(0) - 1)
    def _():
        best = jnp.max(m_ref[...], axis=0, keepdims=True)
        st_ref[0:1, :] = best
        st_ref[1:2, :] = jnp.sum(
            s_ref[...] * jnp.exp2((m_ref[...] - best) * kappa), axis=0, keepdims=True
        )


def logits_call(n, kappa, masks, own, far, centroids):
    local_k, width = centroids.shape
    points = 2 * own.shape[0]
    return pl.pallas_call(
        functools.partial(logits_kernel, n, kappa, masks),
        grid=(TILES,),
        in_specs=[whole()] * 3,
        out_specs=[whole()] * 4,
        out_shape=[
            jax.ShapeDtypeStruct((points, width), BF16),
            jax.ShapeDtypeStruct((local_k, points), BF16),
            jax.ShapeDtypeStruct((TILES, points), F32),
            jax.ShapeDtypeStruct((2, points), F32),
        ],
        scratch_shapes=[pltpu.VMEM((TILES, points), F32)],
        compiler_params=pltpu.CompilerParams(vmem_limit_bytes=16 << 20),
        name="logits",
    )(own, far, centroids)


def fetch_kernel(cen_ref, out_ref, sem):
    copy = pltpu.make_async_copy(cen_ref, out_ref, sem)
    copy.start()
    copy.wait()


def fetch_call(centroids):
    return pl.pallas_call(
        fetch_kernel,
        in_specs=[pl.BlockSpec(memory_space=pltpu.HBM)],
        out_specs=whole(),
        out_shape=jax.ShapeDtypeStruct(centroids.shape, centroids.dtype),
        scratch_shapes=[pltpu.SemaphoreType.DMA],
        cost_estimate=pl.CostEstimate(
            flops=0, bytes_accessed=2 * centroids.size * 2, transcendentals=0
        ),
        compiler_params=pltpu.CompilerParams(vmem_limit_bytes=8 << 20),
        name="fetch",
    )(centroids)


def mass_rows(column_masses):
    eye = lax.broadcasted_iota(jnp.int32, column_masses.shape, 0) == lax.broadcasted_iota(
        jnp.int32, column_masses.shape, 1
    )
    return jnp.sum(jnp.where(eye, column_masses, 0.0), axis=0, keepdims=True)


def pack_mass(row, width):
    high = row.astype(BF16).astype(F32)
    low = row - high
    pad = jnp.zeros((1, width - 2 * LANES), F32)
    line = jnp.concatenate([high, low, pad], axis=1)
    return jnp.broadcast_to(line, (SUB, width)).astype(BF16)


def unpack_mass(rows):
    line = rows[0:1, :].astype(F32)
    return line[:, :LANES] + line[:, LANES : 2 * LANES]


def update_kernel(
    n, kappa, heads, asg_any, dup_any, e_ref, cen_ref, x_ref, m_ref, st_ref, one_any, *refs
):
    parts = len(heads) + 1
    sends, keeps = refs[:parts], refs[parts : 2 * parts]
    one_ref, mv_ref, asg_ref, dup_ref, sems, one_sems, *accs = refs[2 * parts :]
    t = pl.program_id(0)
    width = cen_ref.shape[1]
    tk = one_ref.shape[1]
    chunks = width // LANES
    k2 = accs[0].shape[0] // SUB - SUB

    piece = min(1024, asg_ref.shape[0])

    def pieces(c):
        at = pl.ds(pl.multiple_of(c * piece, piece), piece)
        return (
            pltpu.make_async_copy(asg_any.at[at], asg_ref.at[at], sems.at[0, c]),
            pltpu.make_async_copy(dup_any.at[at], dup_ref.at[at], sems.at[1, c]),
        )

    @pl.when(t == 0)
    def _():
        for c in range(asg_ref.shape[0] // piece):
            for copy in pieces(c):
                copy.start()
        for ref in (*accs, mv_ref):
            step = 64 * SUB

            def clear(i, _):
                ref[pl.ds(pl.multiple_of(i * step, step), step), :] = jnp.zeros((step, LANES), F32)
                return _

            lax.fori_loop(0, ref.shape[0] // step, clear, 0)
            done = ref.shape[0] // step * step
            if done < ref.shape[0]:
                ref[done:, :] = jnp.zeros((ref.shape[0] - done, LANES), F32)
        for copy in pieces(0):
            copy.wait()

    old = t - 1

    @pl.when((old > 0) & (lax.rem(old * tk, piece) == 0))
    def _():
        for copy in pieces(lax.div(old * tk, piece)):
            copy.wait()

    def scatter(offsets, dups, rows):
        news = []
        for i, row in enumerate(rows):
            at = pl.ds(pl.multiple_of(offsets[i], SUB), SUB)
            if i >= ACCS:
                row = row + rows[i - ACCS] * dups[i - ACCS]
            news.append((accs[i % ACCS], at, accs[i % ACCS][at, :] + row))
        for ref, at, new in news:
            ref[at, :] = new

    before = pl.ds(pl.multiple_of(jnp.maximum(t - 1, 0) * tk, tk), tk)
    asg_view, dup_view = asg_ref.at[before], dup_ref.at[before]
    for k in range(0, tk, 2 * ACCS):
        group = range(k, k + 2 * ACCS)
        scatter(
            [asg_view[i] for i in group],
            [dup_view[i] for i in group[:ACCS]],
            [mv_ref[i * SUB : (i + 1) * SUB, :] for i in group],
        )

    here = pl.ds(pl.multiple_of(t * tk, tk), tk)
    slot = lax.rem(t, 2)

    def put(tile):
        which = lax.rem(tile, 2)
        to = pl.ds(pl.multiple_of(tile * tk, tk), tk)
        return pltpu.make_async_copy(one_ref.at[which], one_any.at[to], one_sems.at[which])

    @pl.when(t > 1)
    def _():
        put(t - 2).wait()

    factor = jnp.exp2((m_ref[pl.ds(t, 1), :] - st_ref[0:1, :]) * kappa) / st_ref[1:2, :]
    resp = e_ref[here, :].astype(F32) * factor
    mass = jnp.sum(resp, axis=1, keepdims=True)
    weighted = jnp.dot(resp.astype(BF16), x_ref[...], preferred_element_type=F32)
    fresh = (weighted + PRIOR_ONE * cen_ref[here, :].astype(F32)) * (1.0 / (mass + PRIOR_ONE))
    one_ref[slot] = fresh.astype(BF16)
    put(t).start()
    moved = (mass * fresh).astype(BF16).astype(F32)
    for d in range(chunks):
        mv_ref[pl.ds(d, tk, stride=SUB), :] = moved[:, d * LANES : (d + 1) * LANES]
    mv_ref[pl.ds(chunks, tk, stride=SUB), :] = jnp.broadcast_to(mass, (tk, LANES))

    @pl.when(t == pl.num_programs(0) - 1)
    def _():
        unroll = 32

        def last(i, _):
            for u in range(0, unroll, 2 * ACCS):
                group = range(u, u + 2 * ACCS)
                base = t * tk + i * unroll
                scatter(
                    [asg_ref[base + v] for v in group],
                    [dup_ref[base + v] for v in group[:ACCS]],
                    [
                        mv_ref[pl.ds(pl.multiple_of((i * unroll + v) * SUB, SUB), SUB), :]
                        for v in group
                    ],
                )
            return _

        if (TILES - 1) * tk % piece == 0:
            for copy in pieces((TILES - 1) * tk // piece):
                copy.wait()
        lax.fori_loop(0, tk // unroll, last, 0)
        step = 32 * SUB

        def merge(i, _):
            at = pl.ds(pl.multiple_of(i * step, step), step)
            total = accs[0][at, :]
            for ref in accs[1:]:
                total = total + ref[at, :]
            accs[0][at, :] = total
            return _

        if ACCS > 1:
            lax.fori_loop(0, k2 * SUB // step, merge, 0)
        acc_ref = accs[0]
        me = lax.axis_index("cent")
        rows = k2 // n
        tail = rows - sum(heads)
        half = n // 2
        for u in range(half):
            first = (1 - u % 2) * (half // 2) + u // 2
            for outs, low in ((sends, 1), (keeps, 0)):
                base = pl.multiple_of((me ^ (2 * u + low)) * (rows * SUB), SUB)
                at = u * (tail + SUB)
                for d in range(chunks):
                    col = slice(d * LANES, (d + 1) * LANES)
                    part = acc_ref[pl.ds(base + d, rows, stride=SUB), :].astype(BF16)
                    row = 0
                    for ref, size in zip(outs, heads):
                        ref[first * size : (first + 1) * size, col] = part[row : row + size]
                        row += size
                    outs[-1][at : at + tail, col] = part[row:]
                line = mass_rows(acc_ref[pl.ds(base + chunks, rows, stride=SUB), :])
                outs[-1][at + tail : at + tail + SUB, :] = pack_mass(line, width)
        for tile in (TILES - 2, TILES - 1):
            put(tile).wait()


def update_call(n, kappa, k2, heads, assign, e, centroids, x, m, stats):
    local_k, width = centroids.shape
    tk = local_k // TILES
    tail = k2 // n - sum(heads)
    messages = [
        jax.ShapeDtypeStruct((n // 2 * size, width), BF16) for size in (*heads, tail + SUB)
    ] * 2
    offsets = assign * SUB
    meets = (assign == jnp.roll(assign, -ACCS)).astype(F32)
    out = pl.pallas_call(
        functools.partial(update_kernel, n, kappa, heads),
        grid=(TILES,),
        in_specs=[pl.BlockSpec(memory_space=pl.ANY)] * 2 + [whole()] * 5,
        out_specs=[pl.BlockSpec(memory_space=pltpu.HBM)] + [whole()] * len(messages),
        out_shape=[jax.ShapeDtypeStruct((local_k, width), BF16), *messages],
        scratch_shapes=[
            pltpu.VMEM((2, tk, width), BF16),
            pltpu.VMEM(((tk + SUB) * SUB, LANES), F32),
            pltpu.SMEM((local_k,), jnp.int32),
            pltpu.SMEM((local_k,), F32),
            pltpu.SemaphoreType.DMA((2, max(1, local_k // 1024))),
            pltpu.SemaphoreType.DMA((2,)),
            *[pltpu.VMEM(((k2 + SUB) * SUB, LANES), F32)] * ACCS,
        ],
        compiler_params=pltpu.CompilerParams(vmem_limit_bytes=34 << 20),
        name="update",
    )(offsets, meets, e, centroids, x, m, stats)
    parts = len(messages) // 2
    return out[0], out[1 : 1 + parts], out[1 + parts :]


def add_rows(parts, rows):
    total = parts[0][rows, :].astype(F32)
    for ref in parts[1:]:
        total = total + ref[rows, :].astype(F32)
    return total


def add_mass(parts, rows):
    total = unpack_mass(parts[0][rows, :])
    for ref in parts[1:]:
        total = total + unpack_mass(ref[rows, :])
    return total


def head_kernel(count, *refs):
    row = 0
    for ref in refs[count:]:
        size = ref.shape[0]
        ref[...] = add_rows(refs[:count], slice(row, row + size)).astype(BF16)
        row += size


def tail_kernel(count, tail, *refs):
    row = 0
    for ref in refs[count:]:
        for at in range(0, ref.shape[0], tail + SUB):
            end = row + tail
            ref[at : at + tail, :] = add_rows(refs[:count], slice(row, end)).astype(BF16)
            mass = add_mass(refs[:count], slice(end, end + SUB))
            ref[at + tail : at + tail + SUB, :] = pack_mass(mass, ref.shape[1])
            row = end + SUB


def last_kernel(heads, quarter, *refs):
    coarse_ref, *parts = refs[:-1]
    out_ref = refs[-1]
    rows = out_ref.shape[0]
    tail = rows - sum(heads)
    ends = parts[quarter * len(heads) :]
    mass = add_mass(ends, slice(tail, tail + SUB))
    shape = (rows, LANES)
    eye = lax.broadcasted_iota(jnp.int32, shape, 0) == lax.broadcasted_iota(jnp.int32, shape, 1)
    column = jnp.sum(jnp.where(eye, mass, 0.0), axis=1, keepdims=True)
    inverse = 1.0 / (column + PRIOR_TWO)
    row = 0
    for i, size in enumerate((*heads, tail)):
        group = parts[i * quarter : (i + 1) * quarter] if i < len(heads) else ends
        at = slice(row, row + size)
        total = add_rows(group, slice(0, size)) + PRIOR_TWO * coarse_ref[at, :]
        out_ref[at, :] = total * inverse[at]
        row += size


def simple_call(kernel, name, shapes, dtype, *args):
    out = pl.pallas_call(
        kernel,
        in_specs=[whole() for _ in args],
        out_specs=[whole() for _ in shapes],
        out_shape=[jax.ShapeDtypeStruct(s, dtype) for s in shapes],
        compiler_params=pltpu.CompilerParams(vmem_limit_bytes=32 << 20),
        name=name,
    )(*args)
    return out


def shards(n, points, centroids, coarse_init, assign):
    width = points.shape[1]
    rows = coarse_init.shape[0]
    k2 = rows * n
    kappa = math.log2(math.e) / (TEMP * math.sqrt(width))
    own, masks = points, [0]
    groups = [(2 * bit - 1 & ~3,) for bit in powers(8, n)[::-1]] + [(4, 2, 6)]
    for group in groups:
        own = jnp.concatenate([own] + [exchange(own, mask, n) for mask in group])
        masks = masks + [old ^ mask for mask in group for old in masks]
        if group == groups[0]:
            own, centroids = lax.optimization_barrier((own, fetch_call(centroids)))
    far = exchange(own, 1, n)

    x, e, m, stats = logits_call(n, kappa, tuple(masks), own, far, centroids)

    for bit in powers(1, n):
        other = exchange(stats, bit, n)
        top = jnp.maximum(stats[0], other[0])
        total = stats[1] * jnp.exp2((stats[0] - top) * kappa) + other[1] * jnp.exp2(
            (other[0] - top) * kappa
        )
        stats = jnp.stack([top, total])

    heads = (rows * 3 // 8,) * 2 if rows % 128 == 0 else (rows // 2,)
    tail = rows - sum(heads)
    level_one, sends, keeps = update_call(
        n, kappa, k2, heads, assign, e, centroids, x, m, stats
    )

    quarter = n // 4
    zs = [4 * s for s in range(1, quarter)]
    got = exchange(sends[-1], 1, n)
    gots = [exchange(send, 1, n) for send in sends[:-1]]
    tail_sums = functools.partial(tail_kernel, 2, tail)
    block = tail + SUB
    kept, *out = simple_call(
        tail_sums, "tail_z", [(2 * block, width)] * quarter, BF16, keeps[-1], got
    )
    tail_got = [exchange(v, z, n) for v, z in zip(out, zs)]
    firsts = []
    for keep, got, size in zip(keeps, gots, heads):
        out, stay = simple_call(
            functools.partial(head_kernel, 2), "head_y", [(quarter * size, width)] * 2, BF16, keep, got
        )
        firsts.append((stay, exchange(out, 2, n)))
    ends = []
    for (stay, got), size in zip(firsts, heads):
        stay, *out = simple_call(
            functools.partial(head_kernel, 2), "head_z", [(size, width)] * quarter, BF16, stay, got
        )
        ends += [stay] + [exchange(v, z, n) for v, z in zip(out, zs)]
    stay, out = simple_call(
        functools.partial(tail_kernel, quarter, tail), "tail_y", [(block, width)] * 2, BF16,
        kept, *tail_got,
    )
    ends += [stay, exchange(out, 2, n)]
    (level_two,) = simple_call(
        functools.partial(last_kernel, heads, quarter), "last", [(rows, width)], F32,
        coarse_init, *ends,
    )
    return (level_one, level_two)


def solution(mesh):
    n = mesh.shape["cent"]
    both = ("groups", "cent")
    return jax.shard_map(
        functools.partial(shards, n),
        mesh=mesh,
        in_specs=(P(both, None), P(both, None), P(both, None), P(both)),
        out_specs=(P(both, None), P(both, None)),
        check_vma=False,
    )
```
